512 devices in a mesh: row: 32 (over x, z_lo), col: 16 (over y, z_hi, core).
Axes of the slice: x: 4, y: 4, z: 16 (z_hi: 2, z_lo: 8; z = z_hi * 8 + z_lo), core: 2. Of those that a mesh axis runs over, the one named last changes fastest.
Arguments:
- ancestor: float32 [12288, 12288], P('row', 'col'), may hold values from -6 to 6
- pattern: int32 [96, 96], P('row', 'col'), may hold values 0 or 1
- member: int32 [96, 2], replicated, may hold values 0 or 1
- panel: float32 [12288, 512], P('col', 'row'), may hold values from -0.0546875 to 0.0546875
- diag_inv: float32 [256, 512], P(None, 'col'), may hold values from -6 to 6
Outputs:
- ancestor_panel: float32 [12288, 512], P('row', 'col')
- diag_blocks: float32 [256, 512], P(None, 'col')
The draws below stay inside these ranges and needn't reach their ends.
All inputs are finite; a program needn't handle non-finite values. No bound on the sum of `pattern` on one device may be relied on, other than what follows from the above.
Results may differ from the reference program's by a relative error of at most 0.0001.
Values sent between devices are 32-bit elements; how exact they have to be, the bound alone decides.
No kernel may reach another device: no remote copies, remote signals or barrier semaphores. Data moves between devices by JAX's collectives and lax.ppermute only.
A program may use at most 64 MiB of HBM per device.

```python
import jax
import jax.numpy as jnp
from jax import lax

W = 256
BS = 128
NBLK = 96
R = 12288


def with_ends(entries, stream_key, least, largest):
    shape = entries.shape
    index_at = [jax.random.randint(jax.random.fold_in(stream_key, axis), (), 0, shape[axis]) for axis in range(len(shape))]
    entries = entries.at[tuple(index_at)].set(least)
    longest = shape.index(max(shape))
    index_at[longest] = (index_at[longest] + 1) % shape[longest]
    return entries.at[tuple(index_at)].set(largest)


def shard_levels(key, dims, split, low, largest):
    level, own = 1.0, jax.random.fold_in(key, 6)
    for dim, parts in split:
        draws = jnp.exp(jax.random.uniform(jax.random.fold_in(own, dim), (parts,), jnp.float32, low / len(split), largest / len(split)))
        level = level * jnp.repeat(draws, dims[dim] // parts).reshape([-1 if axis == dim else 1 for axis in range(len(dims))])
    return level


def noise(stream_key, extent, scale, most, shards=(), kind=jnp.bfloat16):
    entries = scale * jax.random.normal(stream_key, extent, jnp.float32)
    if shards:
        entries = entries * shard_levels(stream_key, extent, shards, -0.22, 0.18)
    return jnp.clip(entries, -most, most).astype(kind)


def setup_inputs(seed: int = 0) -> dict:
    splits = jax.random.split(jax.random.key(seed), 6)
    return {
        "ancestor": noise(splits[0], (R, R), 1.0, 6.0, ((0, 32), (1, 16)), jnp.float32),
        "pattern": with_ends((jax.random.randint(splits[1], (NBLK, NBLK), 0, 5) < 3).astype(jnp.int32), jax.random.fold_in(splits[1], 1), 0, 1),
        "member": with_ends((jax.random.randint(splits[2], (NBLK, 2), 0, 2) < 1).astype(jnp.int32), jax.random.fold_in(splits[2], 1), 0, 1),
        "panel": noise(splits[3], (R, 2 * W), (BS * NBLK) ** -0.5, 0.0546875, ((0, 16), (1, 32)), jnp.float32),
        "diag_inv": noise(splits[4], (W, 2 * W), 1.0, 6.0, ((1, 16),), jnp.float32),
    }


def reference(ancestor, pattern, member, panel, diag_inv):
    owner = jnp.arange(2 * W) // W
    member_rows = jnp.repeat(member.astype(jnp.float32), BS, axis=0)
    keep_mask = member_rows[:, owner]
    normed = panel * keep_mask

    def block_rows(index):
        strip = lax.dynamic_slice_in_dim(ancestor, index * BS, BS, 0)
        weights = jnp.repeat(pattern[index].astype(jnp.float32), BS)
        return jnp.dot(strip * weights[None, :], normed, precision=lax.Precision.HIGHEST, preferred_element_type=jnp.float32)

    product = lax.map(block_rows, jnp.arange(NBLK, dtype=jnp.int32)).reshape(BS * NBLK, 2 * W)
    ancestor_panel = -(product * keep_mask)
    pieces = []
    for which in range(2):
        lower = which * W
        left = normed[:, lower:lower + W]
        right = ancestor_panel[:, lower:lower + W]
        pieces.append(diag_inv[:, lower:lower + W] - jnp.dot(left.T, right, precision=lax.Precision.HIGHEST, preferred_element_type=jnp.float32))
    diag_blocks = jnp.concatenate(pieces, axis=1)
    return ancestor_panel, diag_blocks
```

```python
import jax
import jax.numpy as jnp
from jax import lax
from jax.sharding import Mesh, PartitionSpec as P

W = 256
BS = 128
ROW = ("x", "zl")
COL = ("y", "zh", "core")
SIZES = (4, 8, 4, 2, 2)
EXACT = lax.Precision.HIGH


def flat(x, zl, y, zh, core):
    return (((x * 8 + zl) * 4 + y) * 2 + zh) * 2 + core


def row_block_pairs():
    pairs = []
    for x in range(4):
        for zl in range(8):
            for y in range(4):
                for zh in range(2):
                    for core in range(2):
                        source = flat(y, zh * 4 + core * 2 + (zl & 1), x, zl >> 2, (zl >> 1) & 1)
                        pairs.append((source, flat(x, zl, y, zh, core)))
    return pairs


def ordered(bit, own, other, axis):
    low = jnp.where(bit == 0, own, other)
    high = jnp.where(bit == 0, other, own)
    return jnp.stack([low, high], axis=axis)


def xor_pairs(size, step):
    return [(i, i ^ step) for i in range(size)]


def keep_rows(member, start, count, which):
    rows = lax.dynamic_slice_in_dim(member, start, count, 0).astype(jnp.float32)
    return jnp.repeat(jnp.where(which == 0, rows[:, 0], rows[:, 1]), BS)


def body(ancestor, pattern, member, panel, diag_inv):
    x, zl = lax.axis_index("x"), lax.axis_index("zl")
    y, zh, core = lax.axis_index("y"), lax.axis_index("zh"), lax.axis_index("core")
    row, col = x * 8 + zl, (y * 2 + zh) * 2 + core
    row_blocks, col_blocks = pattern.shape
    rows, cols = ancestor.shape

    own = panel.T * keep_rows(member, col * col_blocks, col_blocks, x // 2)[None, :]
    part = ordered(zl // 4, own, lax.ppermute(own, "zl", xor_pairs(8, 4)), 0)
    part = ordered(zl // 2 % 2, part, lax.ppermute(part, "zl", xor_pairs(8, 2)), 0)
    part = ordered(zl % 2, part, lax.ppermute(part, "zl", xor_pairs(8, 1)), 2)
    part = part.reshape(128, cols)
    full = lax.all_to_all(jnp.broadcast_to(part[None], (4, 128, cols)), "x", 0, 0, tiled=True)

    half = lax.dynamic_slice(
        full.reshape(4, 2, 2, 32, cols),
        (x // 2 * 2, 0, 0, 0, zl % 2 * rows),
        (2, 2, 2, 32, rows),
    )
    normed_rows = lax.ppermute(
        half.transpose(0, 2, 1, 3, 4).reshape(W, rows), ROW + COL, row_block_pairs()
    )

    weights = pattern.astype(jnp.float32)
    masked = (
        ancestor.reshape(row_blocks, BS, col_blocks, BS) * weights[:, None, :, None]
    ).reshape(rows, cols)
    share = lax.dot_general(
        full.reshape(512, cols),
        masked,
        (((1,), (1,)), ((), ())),
        precision=EXACT,
        preferred_element_type=jnp.float32,
    )
    pieces = lax.all_to_all(share.reshape(8, 64, rows), ("y", "core"), 0, 0, tiled=True)
    summed = pieces.sum(0).reshape(2, 32, rows)
    mine = jnp.where(zh == 0, summed[0], summed[1])
    theirs = jnp.where(zh == 0, summed[1], summed[0])
    product = mine + lax.ppermute(theirs, "zh", xor_pairs(2, 1))
    kept = product * keep_rows(member, row * row_blocks, row_blocks, y // 2)[None, :]

    term = lax.dot_general(
        kept,
        normed_rows,
        (((1,), (1,)), ((), ())),
        precision=EXACT,
        preferred_element_type=jnp.float32,
    )
    owned = lax.all_to_all(term.reshape(32, 1, W), ROW, 0, 0, tiled=True).sum(0)
    total = lax.all_to_all(jnp.broadcast_to(owned[None], (32, 1, W)), ROW, 0, 0, tiled=True)
    diag_out = diag_inv + total.reshape(32, W).T
    return (-kept).T, diag_out


def solution(mesh):
    fine = Mesh(mesh.devices.reshape(SIZES), ROW + COL)
    placed = (P(ROW, COL), P(ROW, COL), P(), P(COL, ROW), P(None, COL))
    return jax.shard_map(
        body,
        mesh=fine,
        in_specs=placed,
        out_specs=(P(ROW, COL), P(None, COL)),
        check_vma=False,
    )
```

```python
import jax
import jax.numpy as jnp
from jax import lax
from jax.sharding import Mesh, PartitionSpec as P


W = 256
BS = 128
ROW = ("x", "zl")
COL = ("y", "zh", "core")
SIZES = (4, 8, 4, 2, 2)
CLOSE = lax.Precision.HIGH


def flat(x, zl, y, zh, core):
    return (((x * 8 + zl) * 4 + y) * 2 + zh) * 2 + core


def row_block_pairs(turn):
    pairs = []
    for x in range(4):
        for zl in range(8):
            for y in range(4):
                for zh in range(2):
                    for core in range(2):
                        source = flat(y ^ turn, zh * 4 + core * 2 + (zl & 1), x, zl >> 2, (zl >> 1) & 1)
                        pairs.append((source, flat(x, zl, y, zh, core)))
    return pairs


def xor_pairs(size, step):
    return [(i, i ^ step) for i in range(size)]


def swapped(bit, first, second):
    return jnp.where(bit == 0, first, second), jnp.where(bit == 0, second, first)


def product(left, right):
    return lax.dot_general(
        left, right, (((1,), (1,)), ((), ())), precision=CLOSE, preferred_element_type=jnp.float32
    )


def copies(block, count, axes):
    return lax.all_to_all(jnp.broadcast_to(block[None], (count,) + block.shape), axes, 0, 0, tiled=True)


def body(ancestor, pattern, member, panel, diag_inv):
    x, zl = lax.axis_index("x"), lax.axis_index("zl")
    y, zh, core = lax.axis_index("y"), lax.axis_index("zh"), lax.axis_index("core")
    row, col = x * 8 + zl, (y * 2 + zh) * 2 + core
    bit2, bit1, bit0 = zl // 4, zl // 2 % 2, zl % 2
    row_blocks, col_blocks = pattern.shape
    rows, cols = ancestor.shape
    share = panel.shape[1]

    own = panel.T
    two = jnp.stack([own, lax.ppermute(own, "zl", xor_pairs(8, 4))])
    four = jnp.stack(swapped(bit1, two, lax.ppermute(two, "zl", xor_pairs(8, 2))))
    other_four = lax.ppermute(four, "zl", xor_pairs(8, 1))

    flags = member.astype(jnp.float32)
    keep_cols = lax.dynamic_slice_in_dim(flags, col * col_blocks, col_blocks, 0).T
    keep_cols = jnp.repeat(keep_cols, BS, axis=1)
    keep_rows = lax.dynamic_slice_in_dim(flags, row * row_blocks, row_blocks, 0)
    keep_rows = jnp.repeat(jnp.where(y // 2 == 0, keep_rows[:, 0], keep_rows[:, 1]), BS)
    weights = pattern.astype(jnp.float32)
    masked = (
        ancestor.reshape(row_blocks, BS, col_blocks, BS) * weights[:, None, :, None]
    ).reshape(rows, cols)

    full = copies(jnp.stack([four, other_four], axis=1).reshape(8 * share, cols), 4, "x")
    full = full.reshape(2, 16 * share, cols) * keep_cols[:, None, :]
    partial_sum = product(full.reshape(32 * share, cols), masked)
    lower, upper = swapped(bit2, four[:, 0], four[:, 1])
    other_lower, other_upper = swapped(bit2, other_four[:, 0], other_four[:, 1])
    lower = jnp.stack(swapped(bit0, lower, other_lower), axis=1)
    upper = jnp.stack(swapped(bit0, upper, other_upper), axis=1)
    ordered = jnp.stack([lower, upper]).reshape(8 * share, cols)
    half = lax.dynamic_slice_in_dim(ordered, bit0 * rows, rows, 1)
    normed = []
    for turn in (0, 1):
        normed.append(lax.ppermute(half, ROW + COL, row_block_pairs(turn)))

    pieces = partial_sum.reshape(8, 4 * share, rows)
    pieces = lax.all_to_all(pieces, ("y", "core"), 0, 0, tiled=True)
    pieces = pieces.reshape(8, 2, 2, share, rows)
    side = zh ^ bit2
    theirs = lax.dynamic_index_in_dim(pieces, 1 - side, 2, keepdims=False).sum(0).reshape(2 * share, rows)
    mine = lax.dynamic_index_in_dim(pieces, side, 2, keepdims=False).sum(0).reshape(2 * share, rows)
    arrived = lax.ppermute(theirs, "zh", xor_pairs(2, 1))
    def term_of(values):
        values = values * keep_rows[None, :]
        ends = swapped(y % 2, product(values, normed[0]), product(values, normed[1]))
        term = jnp.concatenate(ends, axis=1).reshape(2, share, W)
        return jnp.stack(swapped(bit0, term[0], term[1])).reshape(2 * share, W)

    term = jnp.concatenate(swapped(zh, term_of(mine), term_of(theirs)))
    owned = lax.all_to_all(term.reshape(64, 1, W), ("zh",) + ROW, 0, 0, tiled=True)
    owned = owned.sum(0)
    arrived, owned = lax.optimization_barrier((arrived, owned))
    total = copies(owned, 32, ROW)
    kept = ((mine + arrived) * keep_rows[None, :]).reshape(2, share, rows)
    kept = jnp.stack(swapped(bit0, kept[0], kept[1])).reshape(2 * share, rows)

    return (-kept).T, diag_inv + total.reshape(2 * share, W).T


def solution(mesh):
    fine = Mesh(mesh.devices.reshape(SIZES), ROW + COL)
    placed = (P(ROW, COL), P(ROW, COL), P(), P(COL, ROW), P(None, COL))
    return jax.shard_map(
        body,
        mesh=fine,
        in_specs=placed,
        out_specs=(P(ROW, COL), P(None, COL)),
        check_vma=False,
    )
```

```python
import jax
import jax.numpy as jnp
from jax import lax
from jax.sharding import Mesh, PartitionSpec as P


BS = 128
ROW = ("x", "zl")
COL = ("y", "zh", "core")
SIZES = (4, 8, 4, 2, 2)
CLOSE = lax.Precision.HIGH


def flat(x, zl, y, zh, core):
    return (((x * 8 + zl) * 4 + y) * 2 + zh) * 2 + core


def row_block_pairs():
    pairs = []
    for x in range(4):
        for zl in range(8):
            for y in range(4):
                for zh in range(2):
                    for core in range(2):
                        source = flat(y ^ core, zh * 4 + core * 2 + (zl & 1), x, zl >> 2, (zl >> 1) & 1)
                        pairs.append((source, flat(x, zl, y, zh, core)))
    return pairs


def xor_pairs(size, step):
    return [(i, i ^ step) for i in range(size)]


def swapped(bit, first, second):
    return jnp.where(bit == 0, first, second), jnp.where(bit == 0, second, first)


def product(left, right):
    return lax.dot_general(
        left, right, (((1,), (1,)), ((), ())), precision=CLOSE, preferred_element_type=jnp.float32
    )


def four_sum(term, axis, size):
    one, two, three = (lax.ppermute(term, axis, xor_pairs(size, k)) for k in (1, 2, 3))
    return (term + one) + (two + three)


def copies(block, count, axes):
    return lax.all_to_all(jnp.broadcast_to(block[None], (count,) + block.shape), axes, 0, 0, tiled=True)


def body(ancestor, pattern, member, panel, diag_inv):
    x, zl = lax.axis_index("x"), lax.axis_index("zl")
    y, zh, core = lax.axis_index("y"), lax.axis_index("zh"), lax.axis_index("core")
    row, col = x * 8 + zl, (y * 2 + zh) * 2 + core
    bit2, bit1, bit0 = zl // 4, zl // 2 % 2, zl % 2
    row_blocks, col_blocks = pattern.shape
    rows, cols = ancestor.shape
    share = panel.shape[1]

    own = panel.T
    two = jnp.stack([own, lax.ppermute(own, "zl", xor_pairs(8, 4))])
    four = jnp.stack(swapped(bit1, two, lax.ppermute(two, "zl", xor_pairs(8, 2))))
    other_four = lax.ppermute(four, "zl", xor_pairs(8, 1))

    flags = member.astype(jnp.float32)
    keep_cols = lax.dynamic_slice_in_dim(flags, col * col_blocks, col_blocks, 0).T
    keep_cols = jnp.repeat(keep_cols, BS, axis=1)
    keep_rows = lax.dynamic_slice_in_dim(flags, row * row_blocks, row_blocks, 0)
    keep_rows = jnp.repeat(jnp.where(y // 2 == 0, keep_rows[:, 0], keep_rows[:, 1]), BS)
    weights = pattern.astype(jnp.float32)
    masked = (
        ancestor.reshape(row_blocks, BS, col_blocks, BS) * weights[:, None, :, None]
    ).reshape(rows, cols)

    full = copies(jnp.stack([four, other_four], axis=1).reshape(8 * share, cols), 4, "x")
    full = full.reshape(2, 16 * share, cols) * keep_cols[:, None, :]
    partial_sum = product(full.reshape(32 * share, cols), masked)
    lower, upper = swapped(bit2, four[:, 0], four[:, 1])
    other_lower, other_upper = swapped(bit2, other_four[:, 0], other_four[:, 1])
    lower = jnp.stack(swapped(bit0, lower, other_lower), axis=1)
    upper = jnp.stack(swapped(bit0, upper, other_upper), axis=1)
    ordered = jnp.stack([lower, upper]).reshape(8 * share, cols)
    half = lax.dynamic_slice_in_dim(ordered, bit0 * rows, rows, 1)
    normed = lax.ppermute(half, ROW + COL, row_block_pairs())
    other_normed = lax.ppermute(normed, "core", xor_pairs(2, 1))

    pieces = partial_sum.reshape(8, 4 * share, rows)
    pieces = lax.all_to_all(pieces, ("y", "core"), 0, 0, tiled=True)
    pieces = pieces.reshape(8, 2, 2, share, rows)
    side = zh ^ bit2
    theirs = lax.dynamic_index_in_dim(pieces, 1 - side, 2, keepdims=False).sum(0)
    mine = lax.dynamic_index_in_dim(pieces, side, 2, keepdims=False).sum(0)
    theirs, mine = theirs.reshape(2 * share, rows), mine.reshape(2 * share, rows)
    kept = (mine + lax.ppermute(theirs, "zh", xor_pairs(2, 1))) * keep_rows[None, :]
    kept = kept.reshape(2, share, rows)
    kept = jnp.stack(swapped(bit0, kept[0], kept[1])).reshape(2 * share, rows)

    ends = swapped((y % 2) ^ core, product(kept, normed), product(kept, other_normed))
    term = jnp.concatenate(ends, axis=1)
    term = four_sum(term, "x", 4)
    term = four_sum(term, "zl", 8)
    term = term + lax.ppermute(term, "zl", xor_pairs(8, 4))
    return (-kept).T, diag_inv + term.T


def solution(mesh):
    fine = Mesh(mesh.devices.reshape(SIZES), ROW + COL)
    placed = (P(ROW, COL), P(ROW, COL), P(), P(COL, ROW), P(None, COL))
    return jax.shard_map(
        body,
        mesh=fine,
        in_specs=placed,
        out_specs=(P(ROW, COL), P(None, COL)),
        check_vma=False,
    )
```

```python
import jax
import jax.numpy as jnp
from jax import lax
from jax.sharding import Mesh, PartitionSpec as P


W = 256
BS = 128
ROW = ("x", "zq", "zm", "z0")
COL = ("y", "zh", "core")
SIZES = (4, 2, 2, 2, 4, 2, 2)
CLOSE = lax.Precision.HIGH


def flat(*place):
    index = 0
    for size, at in zip(SIZES, place):
        index = index * size + at
    return index


def row_block_pairs():
    pairs = []
    for target in range(512):
        rest, place = target, []
        for size in reversed(SIZES):
            place.insert(0, rest % size)
            rest //= size
        x, zq, zm, z0, y, zh, core = place
        pairs.append((flat(y ^ core, zh, core, z0, x, zq, zm), target))
    return pairs


def product(left, right):
    return lax.dot_general(
        left, right, (((1,), (1,)), ((), ())), precision=CLOSE, preferred_element_type=jnp.float32
    )


def copies(block, count, axes):
    return lax.all_to_all(jnp.broadcast_to(block[None], (count,) + block.shape), axes, 0, 0, tiled=True)


def body(ancestor, pattern, member, panel, diag_inv):
    at = {name: lax.axis_index(name) for name in ROW + COL}
    y, zh, core, z0 = at["y"], at["zh"], at["core"], at["z0"]
    row = at["x"] * 8 + at["zq"] * 4 + at["zm"] * 2 + z0
    col = (y * 2 + zh) * 2 + core
    row_blocks, col_blocks = pattern.shape
    rows, cols = ancestor.shape
    share = panel.shape[1]

    flags = member.astype(jnp.float32)
    keep_cols = lax.dynamic_slice_in_dim(flags, col * col_blocks, col_blocks, 0).T
    keep_cols = jnp.repeat(keep_cols, BS, axis=1)
    keep_rows = lax.dynamic_slice_in_dim(flags, row * row_blocks, row_blocks, 0)
    keep_rows = jnp.repeat(jnp.where(y // 2 == 0, keep_rows[:, 0], keep_rows[:, 1]), BS)
    weights = pattern.astype(jnp.float32)
    masked = (
        ancestor.reshape(row_blocks, BS, col_blocks, BS) * weights[:, None, :, None]
    ).reshape(rows, cols)

    four = copies(panel.T, 4, ("zq", "zm"))
    full = copies(four.reshape(4 * share, cols), 8, ("x", "z0"))
    kept_cols = full.reshape(2, 16 * share, cols) * keep_cols[:, None, :]
    partial_sum = product(kept_cols.reshape(32 * share, cols), masked)
    pieces = partial_sum.reshape(4, 2, 2, 2, share, rows).transpose(0, 3, 2, 1, 4, 5)
    pieces = lax.all_to_all(
        pieces.reshape(8, 4 * share, rows), ("y", "core"), 0, 0, tiled=True
    )

    half = full.reshape(4, 2, 2, 2, share, cols)
    half = lax.dynamic_slice(half, (at["x"], 0, 0, 0, 0, z0 * rows), (1, 2, 2, 2, share, rows))
    half = half[0].transpose(1, 2, 0, 3, 4).reshape(8 * share, rows)
    normed = lax.ppermute(half, ROW + COL, row_block_pairs())
    other_normed = lax.ppermute(normed, "core", [(0, 1), (1, 0)])

    pieces = pieces.reshape(8, 2, 2 * share, rows)
    theirs = lax.dynamic_index_in_dim(pieces, 1 - zh, 1, keepdims=False).sum(0)
    mine = lax.dynamic_index_in_dim(pieces, zh, 1, keepdims=False).sum(0)
    arrived = lax.ppermute(theirs, "zh", [(0, 1), (1, 0)])
    kept = (mine + arrived) * keep_rows[None, :]

    first, second = product(kept, normed), product(kept, other_normed)
    ahead = (y % 2) ^ core
    term = jnp.concatenate(
        [jnp.where(ahead == 0, first, second), jnp.where(ahead == 0, second, first)], axis=1
    )
    term = copies(term, 8, ("x", "z0")).reshape(8, 2 * share, W).sum(0)
    term = copies(term, 4, ("zq", "zm")).reshape(4, 2 * share, W).sum(0)
    return (-kept).T, diag_inv + term.T


def solution(mesh):
    fine = Mesh(mesh.devices.reshape(SIZES), ROW + COL)
    placed = (P(ROW, COL), P(ROW, COL), P(), P(COL, ROW), P(None, COL))
    return jax.shard_map(
        body,
        mesh=fine,
        in_specs=placed,
        out_specs=(P(ROW, COL), P(None, COL)),
        check_vma=False,
    )
```

```python
import jax
import jax.numpy as jnp
from jax import lax
from jax.sharding import Mesh, PartitionSpec as P


W = 256
BS = 128
ROW = ("x", "zq", "zm", "z0")
COL = ("y", "zh", "core")
SIZES = (4, 2, 2, 2, 4, 2, 2)
CLOSE = lax.Precision.HIGH


def flat(*place):
    index = 0
    for size, at in zip(SIZES, place):
        index = index * size + at
    return index


def row_block_pairs():
    pairs = []
    for target in range(512):
        rest, place = target, []
        for size in reversed(SIZES):
            place.insert(0, rest % size)
            rest //= size
        x, zq, zm, z0, y, zh, core = place
        pairs.append((flat(y ^ core, zh, core, z0, x, zq, zm), target))
    return pairs


def product(left, right):
    return lax.dot_general(
        left, right, (((1,), (1,)), ((), ())), precision=CLOSE, preferred_element_type=jnp.float32
    )


def copies(block, count, axes):
    return lax.all_to_all(jnp.broadcast_to(block[None], (count,) + block.shape), axes, 0, 0, tiled=True)


def body(ancestor, pattern, member, panel, diag_inv):
    at = {name: lax.axis_index(name) for name in ROW + COL}
    y, zh, core, z0 = at["y"], at["zh"], at["core"], at["z0"]
    row = at["x"] * 8 + at["zq"] * 4 + at["zm"] * 2 + z0
    col = (y * 2 + zh) * 2 + core
    row_blocks, col_blocks = pattern.shape
    rows, cols = ancestor.shape
    share = panel.shape[1]

    flags = member.astype(jnp.float32)
    keep_cols = lax.dynamic_slice_in_dim(flags, col * col_blocks, col_blocks, 0).T
    keep_cols = jnp.repeat(keep_cols, BS, axis=1)
    keep_rows = lax.dynamic_slice_in_dim(flags, row * row_blocks, row_blocks, 0)
    keep_rows = jnp.repeat(jnp.where(y // 2 == 0, keep_rows[:, 0], keep_rows[:, 1]), BS)
    weights = pattern.astype(jnp.float32)
    masked = (
        ancestor.reshape(row_blocks, BS, col_blocks, BS) * weights[:, None, :, None]
    ).reshape(rows, cols)

    four = copies(panel.T, 4, ("zq", "zm"))
    full = copies(four.reshape(4 * share, cols), 8, ("x", "z0"))
    sides = full.reshape(8, 2, 2 * share, cols)

    def reduced(side):
        block = lax.dynamic_index_in_dim(sides, side, 1, keepdims=False)
        block = block.reshape(2, 8 * share, cols) * keep_cols[:, None, :]
        partial_sum = product(block.reshape(16 * share, cols), masked)
        pieces = partial_sum.reshape(4, 2, 2, share, rows).transpose(0, 2, 1, 3, 4)
        pieces = lax.all_to_all(pieces.reshape(8, 2 * share, rows), ("y", "core"), 0, 0, tiled=True)
        return pieces

    theirs, mine = reduced(1 - zh), reduced(zh)

    half = full.reshape(4, 2, 2, 2, share, cols)
    half = lax.dynamic_slice(half, (at["x"], 0, 0, 0, 0, z0 * rows), (1, 2, 2, 2, share, rows))
    half = half[0].transpose(1, 2, 0, 3, 4).reshape(8 * share, rows)
    normed = lax.ppermute(half, ROW + COL, row_block_pairs())
    other_normed = lax.ppermute(normed, "core", [(0, 1), (1, 0)])

    theirs = theirs.sum(0)
    arrived = lax.ppermute(theirs, "zh", [(0, 1), (1, 0)])
    kept = (mine.sum(0) + arrived) * keep_rows[None, :]

    first, second = product(kept, normed), product(kept, other_normed)
    ahead = (y % 2) ^ core
    term = jnp.concatenate(
        [jnp.where(ahead == 0, first, second), jnp.where(ahead == 0, second, first)], axis=1
    )
    term = copies(term, 8, ("x", "z0")).reshape(8, 2 * share, W).sum(0)
    term = copies(term, 4, ("zq", "zm")).reshape(4, 2 * share, W).sum(0)
    return (-kept).T, diag_inv + term.T


def solution(mesh):
    fine = Mesh(mesh.devices.reshape(SIZES), ROW + COL)
    placed = (P(ROW, COL), P(ROW, COL), P(), P(COL, ROW), P(None, COL))
    return jax.shard_map(
        body,
        mesh=fine,
        in_specs=placed,
        out_specs=(P(ROW, COL), P(None, COL)),
        check_vma=False,
    )
```

```python
import jax
import jax.numpy as jnp
from jax import lax
from jax.experimental import pallas as pl
from jax.experimental.pallas import tpu as pltpu
from jax.sharding import Mesh, PartitionSpec as P


W = 256
BS = 128
ROW = ("x", "zq", "zm", "z0")
COL = ("y", "zh", "core")
SIZES = (4, 2, 2, 2, 4, 2, 2)
CLOSE = lax.Precision.HIGH
IN_VMEM = pl.BlockSpec(memory_space=pltpu.VMEM)
IN_HBM = pl.BlockSpec(memory_space=pltpu.HBM)
IN_SMEM = pl.BlockSpec(memory_space=pltpu.SMEM)


def pairs_to(source_of):
    pairs = []
    for target in range(512):
        rest, place = target, []
        for size in reversed(SIZES):
            place.insert(0, rest % size)
            rest //= size
        source = 0
        for size, part in zip(SIZES, source_of(*place)):
            source = source * size + part
        pairs.append((source, target))
    return pairs


def send(values, source_of):
    return lax.ppermute(values, ROW + COL, pairs_to(source_of))


def swapped(bit, first, second):
    return [jnp.where(bit == 0, first, second), jnp.where(bit == 0, second, first)]


def parts_of(values):
    high = values.astype(jnp.bfloat16)
    return high, (values - high.astype(jnp.float32)).astype(jnp.bfloat16)


def mask_blocks(pattern_ref, ancestor_ref, out_ref):
    for a in range(pattern_ref.shape[0]):
        for b in range(pattern_ref.shape[1]):
            place = (pl.ds(a * BS, BS), pl.ds(b * BS, BS))
            out_ref[place] = ancestor_ref[place] * pattern_ref[a, b].astype(jnp.float32)


def split_blocks(own_ref, other_ref, high_ref, low_ref):
    for slot, ref in enumerate((own_ref, other_ref)):
        for b in range(ref.shape[1] // BS):
            here = pl.ds(b * BS, BS)
            high_ref[slot, here, :], low_ref[slot, here, :] = parts_of(ref[:, here].T)


def block_product(
    turn_ref, full_hbm, keep_ref, high_hbm, low_hbm, out_ref, full_ref, high_ref, low_ref, sems
):
    turn = turn_ref[0]
    fetched = [pltpu.make_async_copy(full_hbm, full_ref, sems.at[0])]
    for j in range(2):
        for n, (hbm, ref) in enumerate(((high_hbm, high_ref), (low_hbm, low_ref))):
            fetched.append(pltpu.make_async_copy(hbm.at[turn ^ j], ref.at[j], sems.at[1 + 2 * j + n]))
    for copy in fetched:
        copy.start()
    fetched[0].wait()
    total = 0.0
    for j in range(2):
        lines = []
        for x in range(4):
            for zq in range(2):
                for z0 in range(2):
                    block = full_ref[2 * x + z0, pl.ds((2 * zq + j) * 16, 16), :]
                    lines.append(block * keep_ref[pl.ds(2 * j + x // 2, 1), :])
        high, low = parts_of(jnp.concatenate(lines, axis=0))
        fetched[1 + 2 * j].wait()
        fetched[2 + 2 * j].wait()
        for left, right_ref in ((high, high_ref), (high, low_ref), (low, high_ref)):
            total += jnp.dot(left, right_ref[j], preferred_element_type=jnp.float32)
    out_ref[...] = total.reshape(out_ref.shape)


def kernel_call(body, out_shape, in_specs, out_specs, limit, flops, moved, scratch=()):
    return pl.pallas_call(
        body,
        out_shape=out_shape,
        in_specs=in_specs,
        out_specs=out_specs,
        scratch_shapes=scratch,
        compiler_params=pltpu.CompilerParams(vmem_limit_bytes=limit),
        cost_estimate=pl.CostEstimate(flops=flops, bytes_accessed=moved, transcendentals=0),
    )


def product(left, right):
    return lax.dot_general(
        left, right, (((1,), (1,)), ((), ())), precision=CLOSE, preferred_element_type=jnp.float32
    )


def copies(block, count, axes):
    return lax.all_to_all(jnp.broadcast_to(block[None], (count,) + block.shape), axes, 0, 0, tiled=True)


def body(ancestor, pattern, member, panel, diag_inv):
    at = {name: lax.axis_index(name) for name in ROW + COL}
    zq, zm, z0, y, zh, core = (at[name] for name in ("zq", "zm", "z0", "y", "zh", "core"))
    row = at["x"] * 8 + zq * 4 + zm * 2 + z0
    pair = y * 2 + zh
    row_blocks, col_blocks = pattern.shape
    rows, cols = ancestor.shape
    share = panel.shape[1]

    own = panel.T
    taken = [
        [
            send(own, lambda x, zq, zm, z0, y, zh, core: (x, zq ^ i, core, z0, y, zh, zm ^ j))
            for j in range(2)
        ]
        for i in range(2)
    ]
    part = jnp.stack([block for line in taken for block in line]).reshape(4 * share, cols)

    whole = jax.ShapeDtypeStruct((rows, cols), jnp.float32)
    masked = kernel_call(
        mask_blocks, whole, [IN_SMEM, IN_VMEM], IN_VMEM, 8 << 20, 10**6, 2 * 10**6
    )(pattern, ancestor)
    other_masked = lax.ppermute(masked, "core", [(0, 1), (1, 0)])
    split = jax.ShapeDtypeStruct((2, cols, rows), jnp.bfloat16)
    high, low = kernel_call(
        split_blocks,
        (split, split),
        [IN_VMEM, IN_VMEM],
        (IN_VMEM, IN_VMEM),
        16 << 20,
        10**6,
        5 * 10**6,
    )(masked, other_masked)

    flags = member.astype(jnp.float32)
    keep_rows = lax.dynamic_slice_in_dim(flags, row * row_blocks, row_blocks, 0)
    keep_rows = jnp.repeat(jnp.where(y // 2 == 0, keep_rows[:, 0], keep_rows[:, 1]), BS)
    both = lax.dynamic_slice_in_dim(flags, pair * 2 * col_blocks, 2 * col_blocks, 0)
    both = both.reshape(2, col_blocks, 2).transpose(0, 2, 1)
    keep_cols = jnp.repeat(jnp.stack(swapped(zm, both[0], both[1])).reshape(4, col_blocks), BS, axis=1)

    full = copies(part, 8, ("x", "z0"))

    wanted = jnp.stack(swapped(zq, taken[0][0], taken[1][0])).reshape(2 * share, cols)
    near = [
        send(
            lax.dynamic_slice_in_dim(wanted, (z0 ^ t) * rows, rows, 1),
            lambda x, zq, zm, z0, y, zh, core: (y, zh, zm, z0 ^ t, x, zq, core),
        ).reshape(2, share, rows)
        for t in range(2)
    ]
    pieces = kernel_call(
        block_product,
        jax.ShapeDtypeStruct((4, 4 * share, rows), jnp.float32),
        [IN_SMEM, IN_HBM, IN_VMEM, IN_HBM, IN_HBM],
        IN_VMEM,
        62000000,
        900 * 10**6,
        5 * 10**6,
        [
            pltpu.VMEM((8, 4 * share, cols), jnp.float32),
            pltpu.VMEM((2, cols, rows), jnp.bfloat16),
            pltpu.VMEM((2, cols, rows), jnp.bfloat16),
            pltpu.SemaphoreType.DMA((5,)),
        ],
    )((zm ^ core).reshape(1), full, keep_cols, high, low)
    pieces, *near = lax.optimization_barrier((pieces, *near))
    pieces = lax.all_to_all(pieces, "y", 0, 0, tiled=True).reshape(4, 2, 2 * share, rows)
    near = jnp.stack(swapped(z0, near[0], near[1]), axis=1).reshape(4 * share, rows)
    far = lax.ppermute(near, "y", [(i, i ^ 1) for i in range(4)])
    near = jnp.stack(swapped(y % 2, near, far)).reshape(8 * share, rows)
    far = lax.ppermute(near, "core", [(0, 1), (1, 0)])
    normed = jnp.stack(
        swapped(core, near.reshape(4, 2 * share, rows), far.reshape(4, 2 * share, rows)), axis=1
    ).reshape(W, rows)

    theirs = lax.dynamic_index_in_dim(pieces, 1 - (zh ^ zq), 1, keepdims=False).sum(0)
    mine = lax.dynamic_index_in_dim(pieces, zh ^ zq, 1, keepdims=False).sum(0)
    arrived = lax.ppermute(theirs, "zh", [(0, 1), (1, 0)])
    kept = (mine + arrived) * keep_rows[None, :]

    kept, inverse = lax.optimization_barrier((kept, -kept))
    term = product(kept, normed)
    term = copies(term, 8, ("x", "z0")).reshape(8, 2 * share, W).sum(0)
    term = copies(term, 4, ("zq", "zm")).reshape(4, 2 * share, W).sum(0)
    return inverse.T, diag_inv + term.T


def solution(mesh):
    fine = Mesh(mesh.devices.reshape(SIZES), ROW + COL)
    placed = (P(ROW, COL), P(ROW, COL), P(), P(COL, ROW), P(None, COL))
    return jax.shard_map(
        body,
        mesh=fine,
        in_specs=placed,
        out_specs=(P(ROW, COL), P(None, COL)),
        check_vma=False,
    )
```

```python
import jax
import jax.numpy as jnp
from jax import lax
from jax.experimental import pallas as pl
from jax.experimental.pallas import tpu as pltpu
from jax.sharding import Mesh, PartitionSpec as P


W = 256
BS = 128
ROW = ("x", "zq", "zm", "z0")
COL = ("y", "zh", "core")
SIZES = (4, 2, 2, 2, 4, 2, 2)
CLOSE = lax.Precision.HIGH
IN_VMEM = pl.BlockSpec(memory_space=pltpu.VMEM)
IN_HBM = pl.BlockSpec(memory_space=pltpu.HBM)
IN_SMEM = pl.BlockSpec(memory_space=pltpu.SMEM)


def pairs_to(source_of):
    pairs = []
    for target in range(512):
        rest, place = target, []
        for size in reversed(SIZES):
            place.insert(0, rest % size)
            rest //= size
        source = 0
        for size, part in zip(SIZES, source_of(*place)):
            source = source * size + part
        pairs.append((source, target))
    return pairs


def send(values, source_of):
    return lax.ppermute(values, ROW + COL, pairs_to(source_of))


def swapped(bit, first, second):
    return [jnp.where(bit == 0, first, second), jnp.where(bit == 0, second, first)]


def parts_of(values):
    high = values.astype(jnp.bfloat16)
    return high, (values - high.astype(jnp.float32)).astype(jnp.bfloat16)


def mask_blocks(pattern_ref, ancestor_ref, out_ref):
    for a in range(pattern_ref.shape[0]):
        for b in range(pattern_ref.shape[1]):
            place = (pl.ds(a * BS, BS), pl.ds(b * BS, BS))
            out_ref[place] = ancestor_ref[place] * pattern_ref[a, b].astype(jnp.float32)


def split_blocks(own_ref, other_ref, high_ref, low_ref):
    for slot, ref in enumerate((own_ref, other_ref)):
        for b in range(ref.shape[1] // BS):
            here = pl.ds(b * BS, BS)
            high_ref[slot, here, :], low_ref[slot, here, :] = parts_of(ref[:, here].T)


def block_product(
    turn_ref, full_hbm, keep_ref, high_ref, low_hbm, out_ref, full_ref, low_ref, sems
):
    turn = turn_ref[0]

    def fetch_rows(j, zq):
        here = pl.ds((2 * zq + j) * 16, 16)
        return pltpu.make_async_copy(full_hbm.at[:, here], full_ref.at[:, here], sems.at[2 * j + zq])

    row_copies = [[fetch_rows(j, zq) for zq in range(2)] for j in range(2)]
    low_copies = [
        pltpu.make_async_copy(low_hbm.at[turn ^ j], low_ref.at[j], sems.at[4 + j]) for j in range(2)
    ]
    for copy in (*row_copies[0], *row_copies[1], *low_copies):
        copy.start()
    total, highs = 0.0, []
    for j in range(2):
        for copy in row_copies[j]:
            copy.wait()
        lines = []
        for x in range(4):
            for zq in range(2):
                for z0 in range(2):
                    block = full_ref[2 * x + z0, pl.ds((2 * zq + j) * 16, 16), :]
                    lines.append(block * keep_ref[pl.ds(2 * j + x // 2, 1), :])
        high, low = parts_of(jnp.concatenate(lines, axis=0))
        highs.append(high)
        for left in (high, low):
            total += jnp.dot(left, high_ref[turn ^ j], preferred_element_type=jnp.float32)
    for j in range(2):
        low_copies[j].wait()
        total += jnp.dot(highs[j], low_ref[j], preferred_element_type=jnp.float32)
    out_ref[...] = total.reshape(out_ref.shape)


def kernel_call(body, out_shape, in_specs, out_specs, limit, flops, moved, scratch=()):
    return pl.pallas_call(
        body,
        out_shape=out_shape,
        in_specs=in_specs,
        out_specs=out_specs,
        scratch_shapes=scratch,
        compiler_params=pltpu.CompilerParams(vmem_limit_bytes=limit),
        cost_estimate=pl.CostEstimate(flops=flops, bytes_accessed=moved, transcendentals=0),
    )


def product(left, right):
    return lax.dot_general(
        left, right, (((1,), (1,)), ((), ())), precision=CLOSE, preferred_element_type=jnp.float32
    )


def copies(block, count, axes):
    return lax.all_to_all(jnp.broadcast_to(block[None], (count,) + block.shape), axes, 0, 0, tiled=True)


def body(ancestor, pattern, member, panel, diag_inv):
    at = {name: lax.axis_index(name) for name in ROW + COL}
    zq, zm, z0, y, zh, core = (at[name] for name in ("zq", "zm", "z0", "y", "zh", "core"))
    row = at["x"] * 8 + zq * 4 + zm * 2 + z0
    pair = y * 2 + zh
    row_blocks, col_blocks = pattern.shape
    rows, cols = ancestor.shape
    share = panel.shape[1]

    own = panel.T
    taken = [
        [
            send(own, lambda x, zq, zm, z0, y, zh, core: (x, zq ^ i, core, z0, y, zh, zm ^ j))
            for j in range(2)
        ]
        for i in range(2)
    ]
    part = jnp.stack([block for line in taken for block in line]).reshape(4 * share, cols)

    whole = jax.ShapeDtypeStruct((rows, cols), jnp.float32)
    masked = kernel_call(
        mask_blocks, whole, [IN_SMEM, IN_VMEM], IN_VMEM, 8 << 20, 10**6, 2 * 10**6
    )(pattern, ancestor)
    other_masked = lax.ppermute(masked, "core", [(0, 1), (1, 0)])
    split = jax.ShapeDtypeStruct((2, cols, rows), jnp.bfloat16)
    high, low = kernel_call(
        split_blocks,
        (split, split),
        [IN_VMEM, IN_VMEM],
        (IN_VMEM, IN_VMEM),
        16 << 20,
        10**6,
        5 * 10**6,
    )(masked, other_masked)

    flags = member.astype(jnp.float32)
    keep_rows = lax.dynamic_slice_in_dim(flags, row * row_blocks, row_blocks, 0)
    keep_rows = jnp.repeat(jnp.where(y // 2 == 0, keep_rows[:, 0], keep_rows[:, 1]), BS)
    both = lax.dynamic_slice_in_dim(flags, pair * 2 * col_blocks, 2 * col_blocks, 0)
    both = both.reshape(2, col_blocks, 2).transpose(0, 2, 1)
    keep_cols = jnp.repeat(jnp.stack(swapped(zm, both[0], both[1])).reshape(4, col_blocks), BS, axis=1)

    full = copies(part, 8, ("x", "z0"))

    wanted = jnp.stack(swapped(zq, taken[0][0], taken[1][0])).reshape(2 * share, cols)
    near = [
        send(
            lax.dynamic_slice_in_dim(wanted, (z0 ^ t) * rows, rows, 1),
            lambda x, zq, zm, z0, y, zh, core: (y, zh, zm, z0 ^ t, x, zq, core),
        ).reshape(2, share, rows)
        for t in range(2)
    ]
    pieces = kernel_call(
        block_product,
        jax.ShapeDtypeStruct((4, 4 * share, rows), jnp.float32),
        [IN_SMEM, IN_HBM, IN_VMEM, IN_VMEM, IN_HBM],
        IN_VMEM,
        54000000,
        900 * 10**6,
        5 * 10**6,
        [
            pltpu.VMEM((8, 4 * share, cols), jnp.float32),
            pltpu.VMEM((2, cols, rows), jnp.bfloat16),
            pltpu.SemaphoreType.DMA((6,)),
        ],
    )((zm ^ core).reshape(1), full, keep_cols, high, low)
    pieces = lax.all_to_all(pieces, "y", 0, 0, tiled=True).reshape(4, 2, 2 * share, rows)
    near = jnp.stack(swapped(z0, near[0], near[1]), axis=1).reshape(4 * share, rows)
    far = lax.ppermute(near, "y", [(i, i ^ 1) for i in range(4)])
    near = jnp.stack(swapped(y % 2, near, far)).reshape(8 * share, rows)
    far = lax.ppermute(near, "core", [(0, 1), (1, 0)])
    normed = jnp.stack(
        swapped(core, near.reshape(4, 2 * share, rows), far.reshape(4, 2 * share, rows)), axis=1
    ).reshape(W, rows)

    theirs = lax.dynamic_index_in_dim(pieces, 1 - (zh ^ zq), 1, keepdims=False).sum(0)
    mine = lax.dynamic_index_in_dim(pieces, zh ^ zq, 1, keepdims=False).sum(0)
    arrived = lax.ppermute(theirs, "zh", [(0, 1), (1, 0)])
    kept = (mine + arrived) * keep_rows[None, :]

    kept, inverse = lax.optimization_barrier((kept, -kept))
    term = product(kept, normed)
    term = copies(term, 8, ("x", "z0")).reshape(8, 2 * share, W).sum(0)
    far, farther, close = (
        lax.ppermute(term, ("zq", "zm"), [(i, i ^ k) for i in range(4)]) for k in (2, 3, 1)
    )
    term = (term + close) + (far + farther)
    return inverse.T, diag_inv + term.T


def solution(mesh):
    fine = Mesh(mesh.devices.reshape(SIZES), ROW + COL)
    placed = (P(ROW, COL), P(ROW, COL), P(), P(COL, ROW), P(None, COL))
    return jax.shard_map(
        body,
        mesh=fine,
        in_specs=placed,
        out_specs=(P(ROW, COL), P(None, COL)),
        check_vma=False,
    )
```
